32 devices in a mesh: row: 8 (over z, core), col: 4 (over y, x).
Axes of the slice: x: 2, y: 2, z: 4, core: 2. Of those that a mesh axis runs over, the one named last changes fastest.
Arguments:
- patches: bfloat16 [8, 4, 2, 16, 128, 128], P('row', 'col'), as said below
- windows: bfloat16 [8, 4, 2, 16, 36864], P('row', 'col'), as said below
- candidates: int32 [8, 4, 2, 2, 128], P('row', 'col'), may hold values from -32 to 32, as said below
- live: int32 [8, 4, 2], replicated, may hold values from 1 to 16, as said below
- edges: int32 [8, 2, 2820], P('row', None, 'col'), may hold values from 0 to 255, as said below
- stiffness: float32 [8, 2820], P('row', 'col'), may hold values from 0.3 to 3
Outputs:
- matches: float32 [8, 4, 2, 3, 16], P('row', 'col')
- mesh_shift: float32 [8, 4, 2, 256], P('row', 'col')
The draws below stay inside these ranges and needn't reach their ends.
Inputs may be any that keep to these rules, and one draw needn't show every extreme that they name: `candidates`: the candidate shifts of a patch need not be distinct. live[r, c, k] counts the live slots of seam k of tile (r, c): slots 0 to live - 1; the same for all devices. Each tile's springs are the edges of its 16 x 16 vertex grid, horizontal and vertical, and one diagonal of every cell, in any order. `windows`: window k of tile (r, c) serves the seam that tile (r, c-1) (k = 0) or tile (r-1, c) (k = 1) holds as its seam k. `patches`: patch p of seam k is scored against window p of the neighbour.
All inputs are finite; a program needn't handle non-finite values.
Results may differ from the reference program's by a relative error of at most 0.0003.
Values may be sent and summed in bfloat16 or wider, within the bound.
A program may use at most 64 MiB of HBM per device.

```python
import math
import jax
import jax.numpy as jnp
from jax import lax

PATCH = 128
REACH = 32
WIN = 192
NS = 8
P_SIZE = 16
GV = 16
E = 705
ITERS = 3
TILE_ROWS = 8
TILE_COLS = 4


def window_frame(key, flat_index):
    frame_key = jax.random.fold_in(jax.random.fold_in(key, 101), flat_index)
    return jax.random.normal(frame_key, (WIN, WIN), jnp.float32)


def shift_table(key):
    table_total = TILE_ROWS * TILE_COLS * 2 * 2 * P_SIZE * NS
    values = jax.random.randint(jax.random.fold_in(key, 202), (table_total,), -REACH, REACH + 1)
    half_way = table_total // 2
    high_spot = jax.random.randint(jax.random.fold_in(key, 203), (), 0, half_way)
    low_spot = jax.random.randint(jax.random.fold_in(key, 204), (), half_way, table_total)
    values = values.at[high_spot].set(REACH).at[low_spot].set(-REACH)
    return values.reshape(TILE_ROWS, TILE_COLS, 2, 2, P_SIZE * NS).astype(jnp.int32)


def draw_windows(key, part):

    def one_frame(flat_index):
        return window_frame(key, flat_index).astype(jnp.bfloat16).reshape(WIN * WIN)
    frames = lax.map(one_frame, jnp.arange(TILE_ROWS * TILE_COLS * 2 * P_SIZE, dtype=jnp.int32))
    return frames.reshape(TILE_ROWS, TILE_COLS, 2, P_SIZE, WIN * WIN)


def draw_candidates(key, part):
    return shift_table(key)


def draw_patches(key, part):
    shifts = shift_table(key)
    truth = jax.random.randint(jax.random.fold_in(key, 303), (TILE_ROWS, TILE_COLS, 2, P_SIZE), 0, NS)

    def one_patch(flat_index):
        slot_index = flat_index % P_SIZE
        rest_index = flat_index // P_SIZE
        seam = rest_index % 2
        tile_index = rest_index // 2
        tile_row = tile_index // TILE_COLS
        tile_col = tile_index % TILE_COLS
        near_row = (tile_row + seam) % TILE_ROWS
        near_col = (tile_col + 1 - seam) % TILE_COLS
        near_index = ((near_row * TILE_COLS + near_col) * 2 + seam) * P_SIZE + slot_index
        frame_values = window_frame(key, near_index)
        chosen = truth[tile_row, tile_col, seam, slot_index]
        move_y = shifts[tile_row, tile_col, seam, 0, slot_index * NS + chosen]
        move_x = shifts[tile_row, tile_col, seam, 1, slot_index * NS + chosen]
        cropped = lax.dynamic_slice(frame_values, (REACH + move_y, REACH + move_x), (PATCH, PATCH))
        noise = jax.random.normal(jax.random.fold_in(jax.random.fold_in(key, 404), flat_index), (PATCH, PATCH), jnp.float32)
        return (0.8 * cropped + 0.6 * noise).astype(jnp.bfloat16)
    made = lax.map(one_patch, jnp.arange(TILE_ROWS * TILE_COLS * 2 * P_SIZE, dtype=jnp.int32))
    return made.reshape(TILE_ROWS, TILE_COLS, 2, P_SIZE, PATCH, PATCH)


def draw_live(key, part):
    columns = jnp.arange(TILE_COLS, dtype=jnp.int32)
    low_end = max(P_SIZE // 4, 1)
    ramp = low_end + (P_SIZE - low_end) * columns // max(TILE_COLS - 1, 1)
    lowered = jax.random.randint(jax.random.fold_in(key, 505), (TILE_ROWS, TILE_COLS, 2), 0, low_end + 1)
    counts = jnp.clip(ramp[None, :, None] - lowered, 1, P_SIZE)
    top_row = jax.random.randint(jax.random.fold_in(key, 506), (), 0, TILE_ROWS)
    top_col = jax.random.randint(jax.random.fold_in(key, 507), (), 1, TILE_COLS)
    low_row = jax.random.randint(jax.random.fold_in(key, 508), (), 0, TILE_ROWS)
    counts = counts.at[low_row, 0, :].set(1).at[top_row, top_col, :].set(P_SIZE)
    return counts.astype(jnp.int32)


def draw_edges(key, part):
    grid = jnp.arange(GV * GV, dtype=jnp.int32).reshape(GV, GV)
    cells = TILE_ROWS * TILE_COLS
    flip = jax.random.randint(jax.random.fold_in(key, 601), (cells, (GV - 1) * (GV - 1)), 0, 2)
    diag_first = jnp.where(flip == 1, grid[:-1, 1:].reshape(-1)[None, :], grid[:-1, :-1].reshape(-1)[None, :])
    diag_second = jnp.where(flip == 1, grid[1:, :-1].reshape(-1)[None, :], grid[1:, 1:].reshape(-1)[None, :])
    fixed_first = jnp.concatenate([grid[:, :-1].reshape(-1), grid[:-1, :].reshape(-1)])
    fixed_second = jnp.concatenate([grid[:, 1:].reshape(-1), grid[1:, :].reshape(-1)])
    first_ends = jnp.concatenate([jnp.broadcast_to(fixed_first[None, :], (cells, fixed_first.shape[0])), diag_first], axis=1)
    second_ends = jnp.concatenate([jnp.broadcast_to(fixed_second[None, :], (cells, fixed_second.shape[0])), diag_second], axis=1)

    def one_order(order_key):
        return jax.random.permutation(order_key, E)
    orders = jax.vmap(one_order)(jax.random.split(jax.random.fold_in(key, 602), cells))
    first_ends = jnp.take_along_axis(first_ends, orders, axis=1)
    second_ends = jnp.take_along_axis(second_ends, orders, axis=1)
    paired = jnp.stack([first_ends, second_ends], axis=1)
    paired = paired.reshape(TILE_ROWS, TILE_COLS, 2, E).transpose(0, 2, 1, 3)
    return paired.reshape(TILE_ROWS, 2, TILE_COLS * E).astype(jnp.int32)


def block_scale(rng, shape, cuts, low, high):
    gain = 1.0
    for position, blocks in cuts:
        draws = jax.random.uniform(jax.random.fold_in(jax.random.fold_in(rng, 6), position), (blocks,), jnp.float32, low / len(cuts), high / len(cuts))
        gain = gain * jnp.repeat(jnp.exp(draws), shape[position] // blocks).reshape((-1,) + (1,) * (len(shape) - 1 - position))
    return gain


def setup_inputs(seed: int = 0) -> dict:
    splits = jax.random.split(jax.random.key(seed), 7)
    return {
        "patches": draw_patches(jax.random.fold_in(splits[6], 71), 0),
        "windows": draw_windows(jax.random.fold_in(splits[6], 71), 0),
        "candidates": draw_candidates(jax.random.fold_in(splits[6], 71), 0),
        "live": draw_live(jax.random.fold_in(splits[6], 71), 0),
        "edges": draw_edges(jax.random.fold_in(splits[6], 71), 0),
        "stiffness": jnp.clip(jnp.exp(math.log(3.0) - 2.3025851 * jax.random.uniform(splits[5], (TILE_ROWS, TILE_COLS * E), jnp.float32) ** block_scale(splits[5], (TILE_ROWS, TILE_COLS * E), ((0, 8), (1, 4)), -0.2, 0.2)), 0.3, 3.0),
    }


LAMBDA_REG = 0.05
EPSILON = 1e-05
PRECISE = lax.Precision.HIGHEST

def match_block(patch_raw, frames, list_y, list_x):
    patch_size = patch_raw.shape[-1]
    cand_count = list_y.shape[-1]
    pixel_count = float(patch_size * patch_size)
    frame_pixels_all = frames.reshape(frames.shape[0], WIN, WIN)

    def crop_all(frame_pixels, shifts_y, shifts_x):

        def crop_one(move_y, move_x):
            return lax.dynamic_slice(frame_pixels, (REACH + move_y, REACH + move_x), (patch_size, patch_size))
        return jax.vmap(crop_one)(shifts_y, shifts_x)
    cropped = jax.vmap(crop_all)(frame_pixels_all, list_y, list_x)
    unit_plane = jnp.ones((patch_size, patch_size), patch_raw.dtype)
    patch_sum = jnp.einsum('byx,yx->b', patch_raw, unit_plane, preferred_element_type=jnp.float32)
    patch_square = jnp.einsum('byx,byx->b', patch_raw, patch_raw, preferred_element_type=jnp.float32)
    crop_sum = jnp.einsum('bsyx,yx->bs', cropped, unit_plane, preferred_element_type=jnp.float32)
    crop_square = jnp.einsum('bsyx,bsyx->bs', cropped, cropped, preferred_element_type=jnp.float32)
    cross_sum = jnp.einsum('byx,bsyx->bs', patch_raw, cropped, preferred_element_type=jnp.float32)
    patch_mean = patch_sum / pixel_count
    crop_mean = crop_sum / pixel_count
    patch_var = patch_square / pixel_count - patch_mean * patch_mean
    crop_var = crop_square / pixel_count - crop_mean * crop_mean
    cross_mean = cross_sum / pixel_count - patch_mean[:, None] * crop_mean
    correl = cross_mean / jnp.sqrt((patch_var[:, None] + EPSILON) * (crop_var + EPSILON))
    weight = (1.5 + correl) * (1.5 + correl)
    weight_sum = lax.optimization_barrier(jnp.sum(weight, axis=1))
    along_y = lax.optimization_barrier(jnp.sum(weight * list_y.astype(jnp.float32), axis=1)) / (REACH * weight_sum)
    along_x = lax.optimization_barrier(jnp.sum(weight * list_x.astype(jnp.float32), axis=1)) / (REACH * weight_sum)
    return jnp.stack([along_y, along_x, weight_sum / cand_count])

def reference(patches, windows, candidates, live, edges, stiffness):
    rows_all = TILE_ROWS
    cols_all = TILE_COLS
    slots = jnp.arange(P_SIZE)

    def tile_matches(flat_index):
        tile_row = flat_index // cols_all
        tile_col = flat_index % cols_all
        results = []
        for seam in range(2):
            near_row = jnp.minimum(tile_row + seam, rows_all - 1)
            near_col = jnp.minimum(tile_col + 1 - seam, cols_all - 1)
            exists = (tile_row + seam < rows_all) & (tile_col + 1 - seam < cols_all)
            live_count = jnp.where(exists, live[tile_row, tile_col, seam], 0)
            shift_grid = candidates[tile_row, tile_col, seam].reshape(2, P_SIZE, NS)
            scored = match_block(patches[tile_row, tile_col, seam], windows[near_row, near_col, seam], shift_grid[0], shift_grid[1])
            results.append(scored * (slots < live_count).astype(jnp.float32))
        return jnp.stack(results)
    matches = lax.map(tile_matches, jnp.arange(rows_all * cols_all, dtype=jnp.int32))
    matches = matches.reshape(rows_all, cols_all, 2, 3, P_SIZE)
    picker = (jnp.arange(GV)[None, :] == (slots * GV // P_SIZE)[:, None]).astype(jnp.float32)

    def spread(values):
        return jnp.einsum('rcap,pg->rcag', values, picker, precision=PRECISE)

    def sample(values):
        return jnp.einsum('rcag,pg->rcap', values, picker, precision=PRECISE)

    def from_left(values):
        return jnp.concatenate([jnp.zeros_like(values[:, :1]), values[:, :-1]], axis=1)

    def from_right(values):
        return jnp.concatenate([values[:, 1:], jnp.zeros_like(values[:, :1])], axis=1)

    def from_above(values):
        return jnp.concatenate([jnp.zeros_like(values[:1]), values[:-1]], axis=0)

    def from_below(values):
        return jnp.concatenate([values[1:], jnp.zeros_like(values[:1])], axis=0)
    conf_east = matches[:, :, 0, 2][:, :, None]
    conf_south = matches[:, :, 1, 2][:, :, None]
    shift_east = matches[:, :, 0, :2]
    shift_south = matches[:, :, 1, :2]
    conf_west = from_left(conf_east)
    shift_west = from_left(shift_east)
    conf_north = from_above(conf_south)
    shift_north = from_above(shift_south)
    endpoints = edges.reshape(rows_all, 2, cols_all, E).transpose(0, 2, 1, 3)
    spring = stiffness.reshape(rows_all, cols_all, E)

    def intra_tile(flat_field, ends, strength):
        stretch = (flat_field[:, ends[0]] - flat_field[:, ends[1]]) * strength
        return jnp.zeros_like(flat_field).at[:, ends[0]].add(stretch).at[:, ends[1]].add(-stretch)
    intra = jax.vmap(jax.vmap(intra_tile))

    def operate(vector):
        flat_field = vector.reshape(rows_all, cols_all, 2, GV * GV)
        output = (LAMBDA_REG * flat_field + intra(flat_field, endpoints, spring)).reshape(vector.shape)
        output = output.at[..., :, GV - 1].add(spread(conf_east * sample(vector[..., :, GV - 1] - from_right(vector[..., :, 0]))))
        output = output.at[..., :, 0].add(spread(conf_west * sample(vector[..., :, 0] - from_left(vector[..., :, GV - 1]))))
        output = output.at[..., GV - 1, :].add(spread(conf_south * sample(vector[..., GV - 1, :] - from_below(vector[..., 0, :]))))
        output = output.at[..., 0, :].add(spread(conf_north * sample(vector[..., 0, :] - from_above(vector[..., GV - 1, :]))))
        return output
    forcing = jnp.zeros((rows_all, cols_all, 2, GV, GV), jnp.float32)
    forcing = forcing.at[..., :, GV - 1].add(spread(conf_east * shift_east))
    forcing = forcing.at[..., :, 0].add(-spread(conf_west * shift_west))
    forcing = forcing.at[..., GV - 1, :].add(spread(conf_south * shift_south))
    forcing = forcing.at[..., 0, :].add(-spread(conf_north * shift_north))
    solution = jnp.zeros_like(forcing)
    residual = forcing
    direction = forcing
    norm_now = jnp.sum(residual * residual)
    for iteration in range(ITERS):
        applied = operate(direction)
        step_length = norm_now / jnp.sum(direction * applied)
        solution = solution + step_length * direction
        residual = residual - step_length * applied
        norm_next = jnp.sum(residual * residual)
        direction = residual + norm_next / norm_now * direction
        norm_now = norm_next
    return (matches, solution.reshape(rows_all, cols_all, 2, GV * GV))
```

```python
import jax
import jax.numpy as jnp
from jax import lax
from jax.experimental import pallas as pl
from jax.experimental.pallas import tpu as pltpu
from jax.sharding import PartitionSpec as P

REACH = 32
WIN = 192
NS = 8
P_SIZE = 16
GV = 16
ITERS = 3


LAMBDA_REG = 0.05
EPSILON = 1e-05
PRECISE = lax.Precision.HIGHEST


def shifted(x, axis, by):
    length = lax.axis_size(axis)
    pairs = [(i, i + by) for i in range(length) if 0 <= i + by < length]
    return lax.ppermute(x, axis, pairs)


def with_halo(block, sides, width):
    for axis, dim in sides:
        count = lax.axis_size(axis)
        forward = [(i, i + 1) for i in range(count - 1)]
        backward = [(target, source) for source, target in forward]
        low = lax.ppermute(
            lax.slice_in_dim(block, block.shape[dim] - width, None, axis=dim), axis, forward
        )
        high = lax.ppermute(lax.slice_in_dim(block, 0, width, axis=dim), axis, backward)
        block = jnp.concatenate([low, block, high], axis=dim)
    return block


def match_kernel(counts, cands, cand_rows, west, north, frames, out, flat, plane, sums):
    patch_size = west.shape[-1]
    chunks = frames.shape[-1] // 128
    pitch = chunks + 1
    half = patch_size // 2
    lane = lax.broadcasted_iota(jnp.int32, (half, 128), 1)
    pixel_count = float(patch_size * patch_size)

    def fold(values):
        return jnp.sum(values.reshape(half // 8, 8, 128), axis=0)

    for seam in range(2):
        patches = (west, north)[seam]

        def spread_chunk(chunk, carry):
            start = pl.multiple_of(chunk * 128, 128)
            piece = frames[seam, :, pl.ds(start, 128)].astype(jnp.float32)
            flat[pl.ds(chunk, P_SIZE, stride=pitch), :] = piece
            return carry

        lax.fori_loop(0, chunks, spread_chunk, 0, unroll=8)

        def one_patch(slot, carry):
            plane[...] = patches[slot].astype(jnp.float32)
            parts = [plane[pl.ds(parity, half, stride=2), :] for parity in range(2)]
            own_sum = fold(parts[0] + parts[1])
            own_square = fold(parts[0] * parts[0] + parts[1] * parts[1])
            for cand in range(NS):
                index = slot * NS + cand
                row = REACH + cands[seam, 0, index]
                col = REACH + cands[seam, 1, index]
                crop_sum = crop_square = cross_sum = 0.0
                for parity in range(2):
                    place = (row + parity) * WIN + col
                    chunk = slot * pitch + lax.shift_right_logical(place, 7)
                    offset = lax.bitwise_and(place, 127)
                    low = flat[pl.ds(chunk, half, stride=3), :]
                    high = flat[pl.ds(chunk + 1, half, stride=3), :]
                    crop = jnp.where(lane >= offset, low, high)
                    patch = pltpu.roll(plane[pl.ds(parity, half, stride=2), :], offset, 1)
                    crop_sum = crop_sum + fold(crop)
                    crop_square = crop_square + fold(crop * crop)
                    cross_sum = cross_sum + fold(crop * patch)
                spot = pl.ds(pl.multiple_of(index * 8, 8), 8)
                sums[0, spot, :] = crop_sum
                sums[1, spot, :] = crop_square
                sums[2, spot, :] = cross_sum
                sums[3, spot, :] = own_sum
                sums[4, spot, :] = own_square
            return carry

        lax.fori_loop(0, counts[seam], one_patch, 0)

        def total(which):
            values = sums[which, pl.ds(0, P_SIZE * NS, stride=8), :]
            for part in range(1, 8):
                values = values + sums[which, pl.ds(part, P_SIZE * NS, stride=8), :]
            return jnp.sum(values.T, axis=0, keepdims=True) / pixel_count

        crop_mean, crop_square, cross_mean, patch_mean, patch_square = [total(n) for n in range(5)]
        patch_var = patch_square - patch_mean * patch_mean
        crop_var = crop_square - crop_mean * crop_mean
        cross = cross_mean - patch_mean * crop_mean
        correl = cross / jnp.sqrt((patch_var + EPSILON) * (crop_var + EPSILON))
        weight = (1.5 + correl) * (1.5 + correl)
        index = lax.broadcasted_iota(jnp.int32, weight.shape, 1)
        weight = jnp.where(index < counts[seam] * NS, weight, 0.0)
        rows = jnp.concatenate(
            [
                weight * cand_rows[seam, 0:1, :].astype(jnp.float32),
                weight * cand_rows[seam, 1:2, :].astype(jnp.float32),
                weight,
                jnp.zeros((5, P_SIZE * NS), jnp.float32),
            ],
            axis=0,
        )
        group = lax.broadcasted_iota(jnp.int32, (P_SIZE * NS, P_SIZE), 0) // NS
        member = lax.broadcasted_iota(jnp.int32, (P_SIZE * NS, P_SIZE), 1)
        gathered = jnp.dot(
            rows, (group == member).astype(jnp.float32), precision=PRECISE,
            preferred_element_type=jnp.float32,
        )
        weight_sum = gathered[2:3]
        result = jnp.concatenate(
            [gathered[0:2] / (REACH * weight_sum), weight_sum / NS], axis=0
        )
        slot = lax.broadcasted_iota(jnp.int32, result.shape, 1)
        out[seam] = jnp.where(slot < counts[seam], result, 0.0)


def match_call(counts, cands, west, north, frames):
    patch_size = west.shape[-1]
    pitch = frames.shape[-1] // 128 + 1
    smem = pl.BlockSpec(memory_space=pltpu.SMEM)
    vmem = pl.BlockSpec(memory_space=pltpu.VMEM)
    return pl.pallas_call(
        match_kernel,
        out_shape=jax.ShapeDtypeStruct((2, 3, P_SIZE), jnp.float32),
        in_specs=[smem, smem, vmem, vmem, vmem, vmem],
        out_specs=vmem,
        scratch_shapes=[
            pltpu.VMEM((P_SIZE * pitch, 128), jnp.float32),
            pltpu.VMEM((patch_size, patch_size), jnp.float32),
            pltpu.VMEM((5, P_SIZE * NS * 8, 128), jnp.float32),
        ],
        compiler_params=pltpu.CompilerParams(vmem_limit_bytes=40 * 1024 * 1024),
        name="match",
    )(counts, cands, cands, west, north, frames)


def body(patches, windows, candidates, live, edges, stiffness):
    tile_row = lax.axis_index("row")
    tile_col = lax.axis_index("col")
    west_patches = shifted(patches[0, 0, 0], "col", 1)
    north_patches = shifted(patches[0, 0, 1], "row", 1)
    west_cands = shifted(candidates[0, 0, 0], "col", 1)
    north_cands = shifted(candidates[0, 0, 1], "row", 1)
    count_west = jnp.where(tile_col > 0, live[tile_row, jnp.maximum(tile_col - 1, 0), 0], 0)
    count_north = jnp.where(tile_row > 0, live[jnp.maximum(tile_row - 1, 0), tile_col, 1], 0)
    scored = match_call(
        jnp.stack([count_west, count_north]),
        jnp.stack([west_cands, north_cands]),
        west_patches,
        north_patches,
        windows[0, 0],
    )
    from_west = scored[0]
    from_north = scored[1]
    own_east = shifted(from_west, "col", -1)
    own_south = shifted(from_north, "row", -1)
    matches = jnp.stack([own_east, own_south])[None, None]
    slots = jnp.arange(P_SIZE)
    picker = (jnp.arange(GV)[None, :] == (slots * GV // P_SIZE)[:, None]).astype(jnp.float32)
    vertex = jnp.arange(GV * GV)
    incidence = (edges[0, 0][:, None] == vertex[None, :]).astype(jnp.float32) - (
        edges[0, 1][:, None] == vertex[None, :]
    ).astype(jnp.float32)
    spring = stiffness[0]

    def spread(values):
        return jnp.dot(values, picker, precision=PRECISE)

    def sample(values):
        return jnp.dot(values, picker.T, precision=PRECISE)

    conf_east = own_east[2]
    conf_south = own_south[2]
    conf_west = from_west[2]
    conf_north = from_north[2]

    def operate(vector):
        border = with_halo(vector, (("row", 1), ("col", 2)), 1)
        flat_field = vector.reshape(2, GV * GV)
        stretch = jnp.dot(flat_field, incidence.T, precision=PRECISE) * spring
        output = (LAMBDA_REG * flat_field + jnp.dot(stretch, incidence, precision=PRECISE)).reshape(
            2, GV, GV
        )
        output = output.at[:, :, GV - 1].add(
            spread(conf_east * sample(vector[:, :, GV - 1] - border[:, 1:-1, -1]))
        )
        output = output.at[:, :, 0].add(
            spread(conf_west * sample(vector[:, :, 0] - border[:, 1:-1, 0]))
        )
        output = output.at[:, GV - 1, :].add(
            spread(conf_south * sample(vector[:, GV - 1, :] - border[:, -1, 1:-1]))
        )
        output = output.at[:, 0, :].add(
            spread(conf_north * sample(vector[:, 0, :] - border[:, 0, 1:-1]))
        )
        return output

    forcing = jnp.zeros((2, GV, GV), jnp.float32)
    forcing = forcing.at[:, :, GV - 1].add(spread(conf_east * own_east[:2]))
    forcing = forcing.at[:, :, 0].add(-spread(conf_west * from_west[:2]))
    forcing = forcing.at[:, GV - 1, :].add(spread(conf_south * own_south[:2]))
    forcing = forcing.at[:, 0, :].add(-spread(conf_north * from_north[:2]))
    solution = jnp.zeros_like(forcing)
    residual = forcing

    def two_products(values, applied):
        return lax.psum((jnp.sum(values * values), jnp.sum(values * applied)), ("row", "col"))

    applied = operate(residual)
    norm_now, product = two_products(residual, applied)
    step_length = norm_now / product
    direction = residual
    along = applied
    for iteration in range(ITERS):
        solution = solution + step_length * direction
        residual = residual - step_length * along
        if iteration + 1 < ITERS:
            applied = operate(residual)
            norm_next, product = two_products(residual, applied)
            beta_ratio = norm_next / norm_now
            step_length = norm_next / (product - beta_ratio * norm_next / step_length)
            direction = residual + beta_ratio * direction
            along = applied + beta_ratio * along
            norm_now = norm_next
    mesh_shift = solution.reshape(2, GV * GV)[None, None]
    return (matches, mesh_shift)


def solution(mesh):
    return jax.shard_map(
        body,
        mesh=mesh,
        in_specs=(
            P("row", "col", None, None, None, None),
            P("row", "col", None, None, None),
            P("row", "col", None, None, None),
            P(),
            P("row", None, "col"),
            P("row", "col"),
        ),
        out_specs=(P("row", "col", None, None, None), P("row", "col", None, None)),
        check_vma=False,
    )
```

```python
import functools

import jax
import jax.numpy as jnp
from jax import lax
from jax.experimental import pallas as pl
from jax.experimental.pallas import tpu as pltpu
from jax.sharding import PartitionSpec as P

REACH = 32
WIN = 192
NS = 8
P_SIZE = 16
GV = 16
CELLS = GV * GV
ITERS = 3
GAPS = (1, GV, GV + 1, GV - 1)


LAMBDA_REG = 0.05
EPSILON = 1e-05
PRECISE = lax.Precision.HIGHEST


def shifted(x, axis, by):
    length = lax.axis_size(axis)
    pairs = [(i, i + by) for i in range(length) if 0 <= i + by < length]
    return lax.ppermute(x, axis, pairs)


def match_kernel(counts, cands, cand_rows, west, north, frames, out, flat, plane, sums):
    patch_size = west.shape[-1]
    chunks = frames.shape[-1] // 128
    pitch = chunks + 1
    half = patch_size // 2
    lane = lax.broadcasted_iota(jnp.int32, (half, 128), 1)
    pixel_count = float(patch_size * patch_size)

    def fold(values):
        return jnp.sum(values.reshape(half // 8, 8, 128), axis=0)

    for seam in range(2):
        patches = (west, north)[seam]

        def spread_chunk(chunk, carry):
            start = pl.multiple_of(chunk * 128, 128)
            piece = frames[seam, :, pl.ds(start, 128)].astype(jnp.float32)
            flat[pl.ds(chunk, P_SIZE, stride=pitch), :] = piece
            return carry

        lax.fori_loop(0, chunks, spread_chunk, 0, unroll=8)

        def one_patch(slot, carry):
            plane[...] = patches[slot].astype(jnp.float32)
            parts = [plane[pl.ds(parity, half, stride=2), :] for parity in range(2)]
            own_sum = fold(parts[0] + parts[1])
            own_square = fold(parts[0] * parts[0] + parts[1] * parts[1])
            for cand in range(NS):
                index = slot * NS + cand
                row = REACH + cands[seam, 0, index]
                col = REACH + cands[seam, 1, index]
                crop_sum = crop_square = cross_sum = 0.0
                for parity in range(2):
                    place = (row + parity) * WIN + col
                    chunk = slot * pitch + lax.shift_right_logical(place, 7)
                    offset = lax.bitwise_and(place, 127)
                    low = flat[pl.ds(chunk, half, stride=3), :]
                    high = flat[pl.ds(chunk + 1, half, stride=3), :]
                    crop = jnp.where(lane >= offset, low, high)
                    patch = pltpu.roll(plane[pl.ds(parity, half, stride=2), :], offset, 1)
                    crop_sum = crop_sum + fold(crop)
                    crop_square = crop_square + fold(crop * crop)
                    cross_sum = cross_sum + fold(crop * patch)
                spot = pl.ds(pl.multiple_of(index * 8, 8), 8)
                sums[0, spot, :] = crop_sum
                sums[1, spot, :] = crop_square
                sums[2, spot, :] = cross_sum
                sums[3, spot, :] = own_sum
                sums[4, spot, :] = own_square
            return carry

        lax.fori_loop(0, counts[seam], one_patch, 0)

        def total(which):
            values = sums[which, pl.ds(0, P_SIZE * NS, stride=8), :]
            for part in range(1, 8):
                values = values + sums[which, pl.ds(part, P_SIZE * NS, stride=8), :]
            return jnp.sum(values.T, axis=0, keepdims=True) / pixel_count

        crop_mean, crop_square, cross_mean, patch_mean, patch_square = [total(n) for n in range(5)]
        patch_var = patch_square - patch_mean * patch_mean
        crop_var = crop_square - crop_mean * crop_mean
        cross = cross_mean - patch_mean * crop_mean
        correl = cross / jnp.sqrt((patch_var + EPSILON) * (crop_var + EPSILON))
        weight = (1.5 + correl) * (1.5 + correl)
        index = lax.broadcasted_iota(jnp.int32, weight.shape, 1)
        weight = jnp.where(index < counts[seam] * NS, weight, 0.0)
        rows = jnp.concatenate(
            [
                weight * cand_rows[seam, 0:1, :].astype(jnp.float32),
                weight * cand_rows[seam, 1:2, :].astype(jnp.float32),
                weight,
                jnp.zeros((5, P_SIZE * NS), jnp.float32),
            ],
            axis=0,
        )
        group = lax.broadcasted_iota(jnp.int32, (P_SIZE * NS, P_SIZE), 0) // NS
        member = lax.broadcasted_iota(jnp.int32, (P_SIZE * NS, P_SIZE), 1)
        gathered = jnp.dot(
            rows, (group == member).astype(jnp.float32), precision=PRECISE,
            preferred_element_type=jnp.float32,
        )
        weight_sum = gathered[2:3]
        result = jnp.concatenate(
            [gathered[0:2] / (REACH * weight_sum), weight_sum / NS], axis=0
        )
        slot = lax.broadcasted_iota(jnp.int32, result.shape, 1)
        result = jnp.where(slot < counts[seam], result, 0.0)
        result = jnp.concatenate([result, jnp.zeros((5, P_SIZE), jnp.float32)], axis=0)
        source = lax.broadcasted_iota(jnp.int32, (P_SIZE, CELLS + 128), 0)
        target = lax.broadcasted_iota(jnp.int32, (P_SIZE, CELLS + 128), 1)
        stride = (GV, 1)[seam]
        picked = (target == source * stride) | (target == source + CELLS)
        out[seam] = jnp.dot(
            result, picked.astype(jnp.float32), precision=PRECISE,
            preferred_element_type=jnp.float32,
        )


def match_call(counts, cands, west, north, frames):
    patch_size = west.shape[-1]
    pitch = frames.shape[-1] // 128 + 1
    smem = pl.BlockSpec(memory_space=pltpu.SMEM)
    vmem = pl.BlockSpec(memory_space=pltpu.VMEM)
    return pl.pallas_call(
        match_kernel,
        out_shape=jax.ShapeDtypeStruct((2, 8, CELLS + 128), jnp.float32),
        in_specs=[smem, smem, vmem, vmem, vmem, vmem],
        out_specs=vmem,
        scratch_shapes=[
            pltpu.VMEM((P_SIZE * pitch, 128), jnp.float32),
            pltpu.VMEM((patch_size, patch_size), jnp.float32),
            pltpu.VMEM((5, P_SIZE * NS * 8, 128), jnp.float32),
        ],
        compiler_params=pltpu.CompilerParams(vmem_limit_bytes=40 * 1024 * 1024),
        name="match",
    )(counts, cands, cands, west, north, frames)


def mesh_kernel(
    sizes, scored, springs, matches, shift, back, halo, sent, part, row_parts, col_parts,
    back_send, back_recv, halo_send, halo_recv, row_send, row_recv, col_send, col_recv,
):
    rows, cols = sizes
    me_row = lax.axis_index("row")
    me_col = lax.axis_index("col")

    barrier = pltpu.get_barrier_semaphore()
    for name, count, me in (("row", rows, me_row), ("col", cols, me_col)):
        for step in range(1, count):
            pl.semaphore_signal(
                barrier, inc=1, device_id={name: lax.rem(me + step, count)},
                device_id_type=pl.DeviceIdType.MESH,
            )
    pl.semaphore_wait(barrier, rows + cols - 2)

    has = (me_col < cols - 1, me_row < rows - 1, me_col > 0, me_row > 0)
    there = ({"col": me_col + 1}, {"row": me_row + 1}, {"col": me_col - 1}, {"row": me_row - 1})

    for side in range(2):
        @pl.when(jnp.logical_not(has[side]))
        def _():
            back[side] = jnp.zeros(back.shape[1:], jnp.float32)

    for side in range(4):
        @pl.when(jnp.logical_not(has[side]))
        def _():
            for turn in range(ITERS):
                halo[turn, side] = jnp.zeros(halo.shape[2:], jnp.float32)

    def back_copy(seam):
        return pltpu.make_async_remote_copy(
            src_ref=scored.at[seam], dst_ref=back.at[seam],
            send_sem=back_send.at[seam], recv_sem=back_recv.at[seam],
            device_id=there[seam + 2], device_id_type=pl.DeviceIdType.MESH,
        )

    for seam in range(2):
        @pl.when(has[seam + 2])
        def _():
            back_copy(seam).start()

    for seam in range(2):
        @pl.when(has[seam + 2])
        def _():
            back_copy(seam).wait_send()

        @pl.when(has[seam])
        def _():
            back_copy(seam).wait_recv()

    def halo_copy(turn, side):
        return pltpu.make_async_remote_copy(
            src_ref=sent.at[turn], dst_ref=halo.at[turn, (side + 2) % 4],
            send_sem=halo_send.at[turn, side], recv_sem=halo_recv.at[turn, (side + 2) % 4],
            device_id=there[side], device_id_type=pl.DeviceIdType.MESH,
        )

    def row_copy(turn, step):
        return pltpu.make_async_remote_copy(
            src_ref=part.at[turn, 0], dst_ref=row_parts.at[turn, step - 1],
            send_sem=row_send.at[turn, step - 1], recv_sem=row_recv.at[turn, step - 1],
            device_id={"row": lax.rem(me_row + step, rows)},
            device_id_type=pl.DeviceIdType.MESH,
        )

    def col_copy(turn, step):
        return pltpu.make_async_remote_copy(
            src_ref=part.at[turn, 1], dst_ref=col_parts.at[turn, step - 1],
            send_sem=col_send.at[turn, step - 1], recv_sem=col_recv.at[turn, step - 1],
            device_id={"col": lax.rem(me_col + step, cols)},
            device_id_type=pl.DeviceIdType.MESH,
        )

    east = pltpu.roll(back[0, :, :CELLS], GV - 1, 1)
    south = pltpu.roll(back[1, :, :CELLS], CELLS - GV, 1)
    west = scored[0, :, :CELLS]
    north = scored[1, :, :CELLS]
    for seam in range(2):
        matches[seam] = back[seam, :3, CELLS : CELLS + P_SIZE]
    confs = [side[2:3, :] for side in (east, south, west, north)]
    turns = (GV - 1, CELLS - GV, CELLS - GV + 1, GV)
    component = lax.broadcasted_iota(jnp.int32, (8, CELLS), 0)
    forcing = confs[0] * east + confs[1] * south - confs[2] * west - confs[3] * north
    forcing = jnp.where(component < 2, forcing, 0.0)

    def operate(turn, vector):
        sent[turn] = vector
        for side in range(4):
            @pl.when(has[side])
            def _():
                halo_copy(turn, side).start()
        output = LAMBDA_REG * vector
        for index, gap in enumerate(GAPS):
            pull = springs[index : index + 1, :] * (vector - pltpu.roll(vector, CELLS - gap, 1))
            output = output + pull - pltpu.roll(pull, gap, 1)
        for side in range(4):
            @pl.when(has[side])
            def _():
                halo_copy(turn, side).wait_send()
                halo_copy(turn, (side + 2) % 4).wait_recv()
        for side in range(4):
            border = pltpu.roll(halo[turn, side], turns[side], 1)
            output = output + confs[side] * (vector - border)
        return output

    def lanes(values):
        folded = values[:, :128] + values[:, 128:]
        return jnp.sum(folded, axis=0, keepdims=True)

    def two_products(turn, values, applied):
        total = jnp.concatenate(
            [lanes(values * values), lanes(values * applied), jnp.zeros((6, 128), jnp.float32)],
            axis=0,
        )
        part[turn, 0] = total
        for step in range(1, rows):
            row_copy(turn, step).start()
        for step in range(1, rows):
            row_copy(turn, step).wait()
            total = total + row_parts[turn, step - 1]
        part[turn, 1] = total
        for step in range(1, cols):
            col_copy(turn, step).start()
        for step in range(1, cols):
            col_copy(turn, step).wait()
            total = total + col_parts[turn, step - 1]
        summed = jnp.sum(total, axis=1, keepdims=True)
        return summed[0:1], summed[1:2]

    residual = forcing
    applied = operate(0, residual)
    norm_now, product = two_products(0, residual, applied)
    step_length = norm_now / product
    direction = residual
    along = applied
    answer = jnp.zeros_like(forcing)
    for iteration in range(ITERS):
        answer = answer + step_length * direction
        if iteration + 1 < ITERS:
            residual = residual - step_length * along
            applied = operate(iteration + 1, residual)
            norm_next, product = two_products(iteration + 1, residual, applied)
            beta_ratio = norm_next / norm_now
            step_length = norm_next / (product - beta_ratio * norm_next / step_length)
            direction = residual + beta_ratio * direction
            along = applied + beta_ratio * along
            norm_now = norm_next
    shift[...] = answer[:2]


def mesh_call(scored, springs):
    rows = lax.axis_size("row")
    cols = lax.axis_size("col")
    vmem = pl.BlockSpec(memory_space=pltpu.VMEM)
    dma = pltpu.SemaphoreType.DMA
    return pl.pallas_call(
        functools.partial(mesh_kernel, (rows, cols)),
        out_shape=(
            jax.ShapeDtypeStruct((2, 3, P_SIZE), jnp.float32),
            jax.ShapeDtypeStruct((2, CELLS), jnp.float32),
        ),
        in_specs=[vmem, vmem],
        out_specs=(vmem, vmem),
        scratch_shapes=[
            pltpu.VMEM((2, 8, CELLS + 128), jnp.float32),
            pltpu.VMEM((ITERS, 4, 8, CELLS), jnp.float32),
            pltpu.VMEM((ITERS, 8, CELLS), jnp.float32),
            pltpu.VMEM((ITERS, 2, 8, 128), jnp.float32),
            pltpu.VMEM((ITERS, rows - 1, 8, 128), jnp.float32),
            pltpu.VMEM((ITERS, cols - 1, 8, 128), jnp.float32),
            dma((2,)),
            dma((2,)),
            dma((ITERS, 4)),
            dma((ITERS, 4)),
            dma((ITERS, rows - 1)),
            dma((ITERS, rows - 1)),
            dma((ITERS, cols - 1)),
            dma((ITERS, cols - 1)),
        ],
        compiler_params=pltpu.CompilerParams(collective_id=0, has_side_effects=True),
        name="mesh",
    )(scored, springs)


def body(patches, windows, candidates, live, edges, stiffness):
    tile_row = lax.axis_index("row")
    tile_col = lax.axis_index("col")
    west_patches = shifted(patches[0, 0, 0], "col", 1)
    north_patches = shifted(patches[0, 0, 1], "row", 1)
    west_cands = shifted(candidates[0, 0, 0], "col", 1)
    north_cands = shifted(candidates[0, 0, 1], "row", 1)
    count_west = jnp.where(tile_col > 0, live[tile_row, jnp.maximum(tile_col - 1, 0), 0], 0)
    count_north = jnp.where(tile_row > 0, live[jnp.maximum(tile_row - 1, 0), tile_col, 1], 0)
    scored = match_call(
        jnp.stack([count_west, count_north]),
        jnp.stack([west_cands, north_cands]),
        west_patches,
        north_patches,
        windows[0, 0],
    )
    lower = jnp.minimum(edges[0, 0], edges[0, 1])
    gap = jnp.abs(edges[0, 0] - edges[0, 1])
    classes = jnp.array(GAPS + (0,) * 4)
    spring = jnp.where(gap[None, :] == classes[:, None], stiffness, 0.0)
    starts = (lower[:, None] == jnp.arange(CELLS)[None, :]).astype(jnp.float32)
    springs = jnp.dot(spring, starts, precision=PRECISE)
    matches, mesh_shift = mesh_call(scored, springs)
    return (matches[None, None], mesh_shift[None, None])


def solution(mesh):
    return jax.shard_map(
        body,
        mesh=mesh,
        in_specs=(
            P("row", "col", None, None, None, None),
            P("row", "col", None, None, None),
            P("row", "col", None, None, None),
            P(),
            P("row", None, "col"),
            P("row", "col"),
        ),
        out_specs=(P("row", "col", None, None, None), P("row", "col", None, None)),
        check_vma=False,
    )
```

```python
import functools

import jax
import jax.numpy as jnp
from jax import lax
from jax.experimental import pallas as pl
from jax.experimental.pallas import tpu as pltpu
from jax.sharding import PartitionSpec as P

REACH = 32
WIN = 192
NS = 8
P_SIZE = 16
GV = 16
CELLS = GV * GV
ITERS = 3
GAPS = (1, GV, GV + 1, GV - 1)


LAMBDA_REG = 0.05
CENTER = 8.0
SPAN = 8.0
EPSILON = 1e-05
PRECISE = lax.Precision.HIGHEST


def pass_kernel(sizes, patches, cands, patches_out, cands_out, send, recv):
    rows, cols = sizes
    me_row = lax.axis_index("row")
    me_col = lax.axis_index("col")
    gives = (me_col < cols - 1, me_row < rows - 1)
    takes = (me_col > 0, me_row > 0)
    ahead = ({"col": me_col + 1}, {"row": me_row + 1})
    behind = ({"col": me_col - 1}, {"row": me_row - 1})
    barrier = pltpu.get_barrier_semaphore()
    for flags, where in ((gives, ahead), (takes, behind)):
        for seam in range(2):
            @pl.when(flags[seam])
            def _():
                pl.semaphore_signal(
                    barrier, inc=1, device_id=where[seam], device_id_type=pl.DeviceIdType.MESH
                )
    pl.semaphore_wait(barrier, sum(flag.astype(jnp.int32) for flag in gives + takes))

    def copies(seam):
        return [
            pltpu.make_async_remote_copy(
                src_ref=source.at[seam], dst_ref=target.at[seam],
                send_sem=send.at[seam, which], recv_sem=recv.at[seam, which],
                device_id=ahead[seam], device_id_type=pl.DeviceIdType.MESH,
            )
            for which, (source, target) in enumerate(
                ((cands, cands_out), (patches, patches_out))
            )
        ]

    for seam in range(2):
        @pl.when(gives[seam])
        def _():
            for copy in copies(seam):
                copy.start()

    for seam in range(2):
        @pl.when(gives[seam])
        def _():
            for copy in copies(seam):
                copy.wait_send()

        @pl.when(takes[seam])
        def _():
            for copy in copies(seam):
                copy.wait_recv()


def pass_call(patches, cands):
    anywhere = pl.BlockSpec(memory_space=pl.ANY)
    dma = pltpu.SemaphoreType.DMA
    return pl.pallas_call(
        functools.partial(pass_kernel, (lax.axis_size("row"), lax.axis_size("col"))),
        out_shape=(
            jax.ShapeDtypeStruct(patches.shape, patches.dtype),
            jax.ShapeDtypeStruct(cands.shape, cands.dtype),
        ),
        in_specs=[anywhere, anywhere],
        out_specs=(anywhere, anywhere),
        scratch_shapes=[dma((2, 2)), dma((2, 2))],
        compiler_params=pltpu.CompilerParams(collective_id=1, has_side_effects=True),
        name="hand_over",
    )(patches, cands)


def match_kernel(live, cands, cand_rows, patches, frames, out, flat, plane, sums):
    me_row = lax.axis_index("row")
    me_col = lax.axis_index("col")
    counts = (
        jnp.where(me_col > 0, live[me_row, jnp.maximum(me_col - 1, 0), 0], 0),
        jnp.where(me_row > 0, live[jnp.maximum(me_row - 1, 0), me_col, 1], 0),
    )
    patch_size = patches.shape[-1]
    chunks = frames.shape[-1] // 128
    pitch = chunks + 1
    half = patch_size // 2
    lane = lax.broadcasted_iota(jnp.int32, (half, 128), 1)
    pixel_count = float(patch_size * patch_size)

    def fold(values):
        return jnp.sum(values.reshape(half // 8, 8, 128), axis=0)

    for seam in range(2):
        def spread_chunk(chunk, carry):
            start = pl.multiple_of(chunk * 128, 128)
            piece = frames[seam, :, pl.ds(start, 128)].astype(jnp.float32)
            flat[pl.ds(chunk, P_SIZE, stride=pitch), :] = piece
            return carry

        lax.fori_loop(0, chunks, spread_chunk, 0, unroll=8)

        def one_patch(slot, carry):
            plane[...] = patches[seam, slot].astype(jnp.float32)
            parts = [plane[pl.ds(parity, half, stride=2), :] for parity in range(2)]
            own_sum = fold(parts[0] + parts[1])
            own_square = fold(parts[0] * parts[0] + parts[1] * parts[1])
            for cand in range(NS):
                index = slot * NS + cand
                row = REACH + cands[seam, 0, index]
                col = REACH + cands[seam, 1, index]
                crop_sum = crop_square = cross_sum = 0.0
                for parity in range(2):
                    place = (row + parity) * WIN + col
                    chunk = slot * pitch + lax.shift_right_logical(place, 7)
                    offset = lax.bitwise_and(place, 127)
                    low = flat[pl.ds(chunk, half, stride=3), :]
                    high = flat[pl.ds(chunk + 1, half, stride=3), :]
                    crop = jnp.where(lane >= offset, low, high)
                    patch = pltpu.roll(plane[pl.ds(parity, half, stride=2), :], offset, 1)
                    crop_sum = crop_sum + fold(crop)
                    crop_square = crop_square + fold(crop * crop)
                    cross_sum = cross_sum + fold(crop * patch)
                spot = pl.ds(pl.multiple_of(index * 8, 8), 8)
                sums[0, spot, :] = crop_sum
                sums[1, spot, :] = crop_square
                sums[2, spot, :] = cross_sum
                sums[3, spot, :] = own_sum
                sums[4, spot, :] = own_square
            return carry

        lax.fori_loop(0, counts[seam], one_patch, 0)

        def total(which):
            values = sums[which, pl.ds(0, P_SIZE * NS, stride=8), :]
            for part in range(1, 8):
                values = values + sums[which, pl.ds(part, P_SIZE * NS, stride=8), :]
            return jnp.sum(values.T, axis=0, keepdims=True) / pixel_count

        crop_mean, crop_square, cross_mean, patch_mean, patch_square = [total(n) for n in range(5)]
        patch_var = patch_square - patch_mean * patch_mean
        crop_var = crop_square - crop_mean * crop_mean
        cross = cross_mean - patch_mean * crop_mean
        correl = cross / jnp.sqrt((patch_var + EPSILON) * (crop_var + EPSILON))
        weight = (1.5 + correl) * (1.5 + correl)
        index = lax.broadcasted_iota(jnp.int32, weight.shape, 1)
        weight = jnp.where(index < counts[seam] * NS, weight, 0.0)
        rows = jnp.concatenate(
            [
                weight * cand_rows[seam, 0:1, :].astype(jnp.float32),
                weight * cand_rows[seam, 1:2, :].astype(jnp.float32),
                weight,
                jnp.zeros((5, P_SIZE * NS), jnp.float32),
            ],
            axis=0,
        )
        group = lax.broadcasted_iota(jnp.int32, (P_SIZE * NS, P_SIZE), 0) // NS
        member = lax.broadcasted_iota(jnp.int32, (P_SIZE * NS, P_SIZE), 1)
        gathered = jnp.dot(
            rows, (group == member).astype(jnp.float32), precision=PRECISE,
            preferred_element_type=jnp.float32,
        )
        weight_sum = gathered[2:3]
        result = jnp.concatenate(
            [gathered[0:2] / (REACH * weight_sum), weight_sum / NS], axis=0
        )
        slot = lax.broadcasted_iota(jnp.int32, result.shape, 1)
        result = jnp.where(slot < counts[seam], result, 0.0)
        result = jnp.concatenate([result, jnp.zeros((5, P_SIZE), jnp.float32)], axis=0)
        source = lax.broadcasted_iota(jnp.int32, (P_SIZE, CELLS + 128), 0)
        target = lax.broadcasted_iota(jnp.int32, (P_SIZE, CELLS + 128), 1)
        stride = (GV, 1)[seam]
        picked = (target == source * stride) | (target == source + CELLS)
        out[seam] = jnp.dot(
            result, picked.astype(jnp.float32), precision=PRECISE,
            preferred_element_type=jnp.float32,
        )


def match_call(live, cands, patches, frames):
    patch_size = patches.shape[-1]
    pitch = frames.shape[-1] // 128 + 1
    smem = pl.BlockSpec(memory_space=pltpu.SMEM)
    vmem = pl.BlockSpec(memory_space=pltpu.VMEM)
    return pl.pallas_call(
        match_kernel,
        out_shape=jax.ShapeDtypeStruct((2, 8, CELLS + 128), jnp.float32),
        in_specs=[smem, smem, vmem, vmem, vmem],
        out_specs=vmem,
        scratch_shapes=[
            pltpu.VMEM((P_SIZE * pitch, 128), jnp.float32),
            pltpu.VMEM((patch_size, patch_size), jnp.float32),
            pltpu.VMEM((5, P_SIZE * NS * 8, 128), jnp.float32),
        ],
        compiler_params=pltpu.CompilerParams(vmem_limit_bytes=40 * 1024 * 1024),
        name="match",
    )(live, cands, cands, patches, frames)


def mesh_kernel(
    sizes, scored, springs, matches, shift, back, halo, sent, part, row_parts, col_parts,
    back_send, back_recv, halo_send, halo_recv, row_send, row_recv, col_send, col_recv,
):
    rows, cols = sizes
    me_row = lax.axis_index("row")
    me_col = lax.axis_index("col")

    barrier = pltpu.get_barrier_semaphore()
    for name, count, me in (("row", rows, me_row), ("col", cols, me_col)):
        for step in range(1, count):
            pl.semaphore_signal(
                barrier, inc=1, device_id={name: lax.rem(me + step, count)},
                device_id_type=pl.DeviceIdType.MESH,
            )
    pl.semaphore_wait(barrier, rows + cols - 2)

    has = (me_col < cols - 1, me_row < rows - 1, me_col > 0, me_row > 0)
    there = ({"col": me_col + 1}, {"row": me_row + 1}, {"col": me_col - 1}, {"row": me_row - 1})

    for side in range(2):
        @pl.when(jnp.logical_not(has[side]))
        def _():
            back[side] = jnp.zeros(back.shape[1:], jnp.float32)

    for side in range(4):
        @pl.when(jnp.logical_not(has[side]))
        def _():
            for turn in range(ITERS):
                halo[turn, side] = jnp.zeros(halo.shape[2:], jnp.float32)

    def back_copy(seam):
        return pltpu.make_async_remote_copy(
            src_ref=scored.at[seam], dst_ref=back.at[seam],
            send_sem=back_send.at[seam], recv_sem=back_recv.at[seam],
            device_id=there[seam + 2], device_id_type=pl.DeviceIdType.MESH,
        )

    for seam in range(2):
        @pl.when(has[seam + 2])
        def _():
            back_copy(seam).start()

    for seam in range(2):
        @pl.when(has[seam + 2])
        def _():
            back_copy(seam).wait_send()

        @pl.when(has[seam])
        def _():
            back_copy(seam).wait_recv()

    def halo_copy(turn, side):
        return pltpu.make_async_remote_copy(
            src_ref=sent.at[turn], dst_ref=halo.at[turn, (side + 2) % 4],
            send_sem=halo_send.at[turn, side], recv_sem=halo_recv.at[turn, (side + 2) % 4],
            device_id=there[side], device_id_type=pl.DeviceIdType.MESH,
        )

    def row_copy(step):
        return pltpu.make_async_remote_copy(
            src_ref=part.at[0], dst_ref=row_parts.at[step - 1],
            send_sem=row_send.at[step - 1], recv_sem=row_recv.at[step - 1],
            device_id={"row": lax.rem(me_row + step, rows)},
            device_id_type=pl.DeviceIdType.MESH,
        )

    def col_copy(step):
        return pltpu.make_async_remote_copy(
            src_ref=part.at[1], dst_ref=col_parts.at[step - 1],
            send_sem=col_send.at[step - 1], recv_sem=col_recv.at[step - 1],
            device_id={"col": lax.rem(me_col + step, cols)},
            device_id_type=pl.DeviceIdType.MESH,
        )

    east = pltpu.roll(back[0, :, :CELLS], GV - 1, 1)
    south = pltpu.roll(back[1, :, :CELLS], CELLS - GV, 1)
    west = scored[0, :, :CELLS]
    north = scored[1, :, :CELLS]
    for seam in range(2):
        matches[seam] = back[seam, :3, CELLS : CELLS + P_SIZE]
    confs = [side[2:3, :] for side in (east, south, west, north)]
    turns = (GV - 1, CELLS - GV, CELLS - GV + 1, GV)
    component = lax.broadcasted_iota(jnp.int32, (8, CELLS), 0)
    forcing = confs[0] * east + confs[1] * south - confs[2] * west - confs[3] * north
    forcing = jnp.where(component < 2, forcing, 0.0)

    def operate(turn, vector):
        sent[turn] = vector
        for side in range(4):
            @pl.when(has[side])
            def _():
                halo_copy(turn, side).start()
        output = LAMBDA_REG * vector
        for index, gap in enumerate(GAPS):
            pull = springs[index : index + 1, :] * (vector - pltpu.roll(vector, CELLS - gap, 1))
            output = output + pull - pltpu.roll(pull, gap, 1)
        for side in range(4):
            @pl.when(has[side])
            def _():
                halo_copy(turn, side).wait_send()
                halo_copy(turn, (side + 2) % 4).wait_recv()
        for side in range(4):
            border = pltpu.roll(halo[turn, side], turns[side], 1)
            output = output + confs[side] * (vector - border)
        return output

    def lanes(values):
        folded = values[:, :128] + values[:, 128:]
        return jnp.sum(folded, axis=0, keepdims=True)

    basis = [forcing]
    for turn in range(ITERS):
        image = operate(turn, basis[-1])
        basis.append((image - CENTER * basis[-1]) * (1.0 / SPAN))

    pairs = [lanes(basis[(n + 0) // 2] * basis[(n + 1) // 2]) for n in range(2 * ITERS)]
    pad = part.shape[1] - len(pairs)
    total = jnp.concatenate(pairs + [jnp.zeros((pad, 128), jnp.float32)], axis=0)
    part[0] = total
    for step in range(1, rows):
        row_copy(step).start()
    for step in range(1, rows):
        row_copy(step).wait()
        total = total + row_parts[step - 1]
    part[1] = total
    for step in range(1, cols):
        col_copy(step).start()
    for step in range(1, cols):
        col_copy(step).wait()
        total = total + col_parts[step - 1]
    summed = jnp.sum(total, axis=1, keepdims=True)
    moments = [summed[n : n + 1] for n in range(2 * ITERS)]

    def inner(left, right):
        return sum(
            x * y * moments[i + j] for i, x in enumerate(left) for j, y in enumerate(right)
        )

    def apply(terms):
        kept = [CENTER * term for term in terms]
        raised = [SPAN * term for term in terms]
        middle = [low + high for low, high in zip(kept[1:], raised[:-1])]
        return kept[:1] + middle + raised[-1:]

    def combine(left, scale, right):
        joined = [x + scale * y for x, y in zip(left, right)]
        longer = left if len(left) > len(right) else [scale * y for y in right]
        return joined + longer[len(joined) :]

    one = jnp.ones((1, 1), jnp.float32)
    residual = [one]
    direction = [one]
    answer = []
    norm_now = moments[0]
    for iteration in range(ITERS):
        image = apply(direction)
        step_length = norm_now / inner(direction, image)
        answer = combine(answer, step_length, direction)
        if iteration + 1 < ITERS:
            residual = combine(residual, -step_length, image)
            norm_next = inner(residual, residual)
            direction = combine(residual, norm_next / norm_now, direction)
            norm_now = norm_next
    answer = sum(scale * vector for scale, vector in zip(answer, basis))
    shift[...] = answer[:2]


def mesh_call(scored, springs):
    rows = lax.axis_size("row")
    cols = lax.axis_size("col")
    vmem = pl.BlockSpec(memory_space=pltpu.VMEM)
    dma = pltpu.SemaphoreType.DMA
    return pl.pallas_call(
        functools.partial(mesh_kernel, (rows, cols)),
        out_shape=(
            jax.ShapeDtypeStruct((2, 3, P_SIZE), jnp.float32),
            jax.ShapeDtypeStruct((2, CELLS), jnp.float32),
        ),
        in_specs=[vmem, vmem],
        out_specs=(vmem, vmem),
        scratch_shapes=[
            pltpu.VMEM((2, 8, CELLS + 128), jnp.float32),
            pltpu.VMEM((ITERS, 4, 8, CELLS), jnp.float32),
            pltpu.VMEM((ITERS, 8, CELLS), jnp.float32),
            pltpu.VMEM((2, 8, 128), jnp.float32),
            pltpu.VMEM((rows - 1, 8, 128), jnp.float32),
            pltpu.VMEM((cols - 1, 8, 128), jnp.float32),
            dma((2,)),
            dma((2,)),
            dma((ITERS, 4)),
            dma((ITERS, 4)),
            dma((rows - 1,)),
            dma((rows - 1,)),
            dma((cols - 1,)),
            dma((cols - 1,)),
        ],
        compiler_params=pltpu.CompilerParams(collective_id=0, has_side_effects=True),
        name="mesh",
    )(scored, springs)


def body(patches, windows, candidates, live, edges, stiffness):
    given, cands = pass_call(patches[0, 0], candidates[0, 0])
    scored = match_call(live, cands, given, windows[0, 0])
    lower = jnp.minimum(edges[0, 0], edges[0, 1])
    gap = jnp.abs(edges[0, 0] - edges[0, 1])
    classes = jnp.array(GAPS + (0,) * 4)
    spring = jnp.where(gap[None, :] == classes[:, None], stiffness, 0.0)
    starts = (lower[:, None] == jnp.arange(CELLS)[None, :]).astype(jnp.float32)
    springs = jnp.dot(spring, starts, precision=PRECISE)
    matches, mesh_shift = mesh_call(scored, springs)
    return (matches[None, None], mesh_shift[None, None])


def solution(mesh):
    return jax.shard_map(
        body,
        mesh=mesh,
        in_specs=(
            P("row", "col", None, None, None, None),
            P("row", "col", None, None, None),
            P("row", "col", None, None, None),
            P(),
            P("row", None, "col"),
            P("row", "col"),
        ),
        out_specs=(P("row", "col", None, None, None), P("row", "col", None, None)),
        check_vma=False,
    )
```

```python
import functools

import jax
import jax.numpy as jnp
from jax import lax
from jax.experimental import pallas as pl
from jax.experimental.pallas import tpu as pltpu
from jax.sharding import PartitionSpec as P

REACH = 32
WIN = 192
NS = 8
P_SIZE = 16
GV = 16
CELLS = GV * GV
ITERS = 3
GAPS = (1, GV, GV + 1, GV - 1)


LAMBDA_REG = 0.05
CENTER = 8.0
SPAN = 8.0
EPSILON = 1e-05
PRECISE = lax.Precision.HIGHEST


def pass_kernel(sizes, patches, cands, patches_out, cands_out, send, recv):
    rows, cols = sizes
    me_row = lax.axis_index("row")
    me_col = lax.axis_index("col")
    gives = (me_col < cols - 1, me_row < rows - 1)
    takes = (me_col > 0, me_row > 0)
    ahead = ({"col": me_col + 1}, {"row": me_row + 1})
    behind = ({"col": me_col - 1}, {"row": me_row - 1})
    barrier = pltpu.get_barrier_semaphore()
    for flags, where in ((gives, ahead), (takes, behind)):
        for seam in range(2):
            @pl.when(flags[seam])
            def _():
                pl.semaphore_signal(
                    barrier, inc=1, device_id=where[seam], device_id_type=pl.DeviceIdType.MESH
                )
    pl.semaphore_wait(barrier, sum(flag.astype(jnp.int32) for flag in gives + takes))

    def copies(seam):
        return [
            pltpu.make_async_remote_copy(
                src_ref=source.at[seam], dst_ref=target.at[seam],
                send_sem=send.at[seam, which], recv_sem=recv.at[seam, which],
                device_id=ahead[seam], device_id_type=pl.DeviceIdType.MESH,
            )
            for which, (source, target) in enumerate(
                ((cands, cands_out), (patches, patches_out))
            )
        ]

    for seam in range(2):
        @pl.when(gives[seam])
        def _():
            for copy in copies(seam):
                copy.start()

    for seam in range(2):
        @pl.when(gives[seam])
        def _():
            for copy in copies(seam):
                copy.wait_send()

        @pl.when(takes[seam])
        def _():
            for copy in copies(seam):
                copy.wait_recv()


def pass_call(patches, cands):
    anywhere = pl.BlockSpec(memory_space=pl.ANY)
    dma = pltpu.SemaphoreType.DMA
    return pl.pallas_call(
        functools.partial(pass_kernel, (lax.axis_size("row"), lax.axis_size("col"))),
        out_shape=(
            jax.ShapeDtypeStruct(patches.shape, patches.dtype),
            jax.ShapeDtypeStruct(cands.shape, cands.dtype),
        ),
        in_specs=[anywhere, anywhere],
        out_specs=(anywhere, anywhere),
        scratch_shapes=[dma((2, 2)), dma((2, 2))],
        compiler_params=pltpu.CompilerParams(
            collective_id=1, has_side_effects=True, vmem_limit_bytes=4 * 1024 * 1024
        ),
        cost_estimate=pl.CostEstimate(
            flops=0, bytes_accessed=32 * patches.size * patches.dtype.itemsize, transcendentals=0
        ),
        name="hand_over",
    )(patches, cands)


def match_kernel(live, cands, cand_rows, patches, frames, out, flat, plane, sums):
    me_row = lax.axis_index("row")
    me_col = lax.axis_index("col")
    counts = (
        jnp.where(me_col > 0, live[me_row, jnp.maximum(me_col - 1, 0), 0], 0),
        jnp.where(me_row > 0, live[jnp.maximum(me_row - 1, 0), me_col, 1], 0),
    )
    patch_size = patches.shape[-1]
    chunks = frames.shape[-1] // 128
    pitch = chunks + 1
    half = patch_size // 2
    lane = lax.broadcasted_iota(jnp.int32, (half, 128), 1)
    pixel_count = float(patch_size * patch_size)

    def fold(values):
        return jnp.sum(values.reshape(half // 8, 8, 128), axis=0)

    for seam in range(2):
        def spread_chunk(chunk, carry):
            start = pl.multiple_of(chunk * 128, 128)
            piece = frames[seam, :, pl.ds(start, 128)].astype(jnp.float32)
            flat[pl.ds(chunk, P_SIZE, stride=pitch), :] = piece
            return carry

        lax.fori_loop(0, chunks, spread_chunk, 0, unroll=8)

        def one_patch(slot, carry):
            plane[...] = patches[seam, slot].astype(jnp.float32)
            parts = [plane[pl.ds(parity, half, stride=2), :] for parity in range(2)]
            own_sum = fold(parts[0] + parts[1])
            own_square = fold(parts[0] * parts[0] + parts[1] * parts[1])
            for cand in range(NS):
                index = slot * NS + cand
                row = REACH + cands[seam, 0, index]
                col = REACH + cands[seam, 1, index]
                crop_sum = crop_square = cross_sum = 0.0
                for parity in range(2):
                    place = (row + parity) * WIN + col
                    chunk = slot * pitch + lax.shift_right_logical(place, 7)
                    offset = lax.bitwise_and(place, 127)
                    low = flat[pl.ds(chunk, half, stride=3), :]
                    high = flat[pl.ds(chunk + 1, half, stride=3), :]
                    crop = jnp.where(lane >= offset, low, high)
                    patch = pltpu.roll(plane[pl.ds(parity, half, stride=2), :], offset, 1)
                    crop_sum = crop_sum + fold(crop)
                    crop_square = crop_square + fold(crop * crop)
                    cross_sum = cross_sum + fold(crop * patch)
                spot = pl.ds(pl.multiple_of(index * 8, 8), 8)
                sums[0, spot, :] = crop_sum
                sums[1, spot, :] = crop_square
                sums[2, spot, :] = cross_sum
                sums[3, spot, :] = own_sum
                sums[4, spot, :] = own_square
            return carry

        lax.fori_loop(0, counts[seam], one_patch, 0)

        def total(which):
            values = sums[which, pl.ds(0, P_SIZE * NS, stride=8), :]
            for part in range(1, 8):
                values = values + sums[which, pl.ds(part, P_SIZE * NS, stride=8), :]
            return jnp.sum(values.T, axis=0, keepdims=True) / pixel_count

        crop_mean, crop_square, cross_mean, patch_mean, patch_square = [total(n) for n in range(5)]
        patch_var = patch_square - patch_mean * patch_mean
        crop_var = crop_square - crop_mean * crop_mean
        cross = cross_mean - patch_mean * crop_mean
        correl = cross / jnp.sqrt((patch_var + EPSILON) * (crop_var + EPSILON))
        weight = (1.5 + correl) * (1.5 + correl)
        index = lax.broadcasted_iota(jnp.int32, weight.shape, 1)
        weight = jnp.where(index < counts[seam] * NS, weight, 0.0)
        rows = jnp.concatenate(
            [
                weight * cand_rows[seam, 0:1, :].astype(jnp.float32),
                weight * cand_rows[seam, 1:2, :].astype(jnp.float32),
                weight,
                jnp.zeros((5, P_SIZE * NS), jnp.float32),
            ],
            axis=0,
        )
        group = lax.broadcasted_iota(jnp.int32, (P_SIZE * NS, P_SIZE), 0) // NS
        member = lax.broadcasted_iota(jnp.int32, (P_SIZE * NS, P_SIZE), 1)
        gathered = jnp.dot(
            rows, (group == member).astype(jnp.float32), precision=PRECISE,
            preferred_element_type=jnp.float32,
        )
        weight_sum = gathered[2:3]
        result = jnp.concatenate(
            [gathered[0:2] / (REACH * weight_sum), weight_sum / NS], axis=0
        )
        slot = lax.broadcasted_iota(jnp.int32, result.shape, 1)
        result = jnp.where(slot < counts[seam], result, 0.0)
        result = jnp.concatenate([result, jnp.zeros((5, P_SIZE), jnp.float32)], axis=0)
        source = lax.broadcasted_iota(jnp.int32, (P_SIZE, CELLS + 128), 0)
        target = lax.broadcasted_iota(jnp.int32, (P_SIZE, CELLS + 128), 1)
        stride = (GV, 1)[seam]
        picked = (target == source * stride) | (target == source + CELLS)
        out[seam] = jnp.dot(
            result, picked.astype(jnp.float32), precision=PRECISE,
            preferred_element_type=jnp.float32,
        )


def match_call(live, cands, patches, frames):
    patch_size = patches.shape[-1]
    pitch = frames.shape[-1] // 128 + 1
    smem = pl.BlockSpec(memory_space=pltpu.SMEM)
    vmem = pl.BlockSpec(memory_space=pltpu.VMEM)
    return pl.pallas_call(
        match_kernel,
        out_shape=jax.ShapeDtypeStruct((2, 8, CELLS + 128), jnp.float32),
        in_specs=[smem, smem, vmem, vmem, vmem],
        out_specs=vmem,
        scratch_shapes=[
            pltpu.VMEM((P_SIZE * pitch, 128), jnp.float32),
            pltpu.VMEM((patch_size, patch_size), jnp.float32),
            pltpu.VMEM((5, P_SIZE * NS * 8, 128), jnp.float32),
        ],
        compiler_params=pltpu.CompilerParams(vmem_limit_bytes=24 * 1024 * 1024),
        name="match",
    )(live, cands, cands, patches, frames)


def mesh_kernel(
    sizes, scored, springs, matches, shift, back, halo, sent, part, row_parts, col_parts,
    back_send, back_recv, halo_send, halo_recv, row_send, row_recv, col_send, col_recv,
):
    rows, cols = sizes
    me_row = lax.axis_index("row")
    me_col = lax.axis_index("col")

    barrier = pltpu.get_barrier_semaphore()
    for name, count, me in (("row", rows, me_row), ("col", cols, me_col)):
        for step in range(1, count):
            pl.semaphore_signal(
                barrier, inc=1, device_id={name: lax.rem(me + step, count)},
                device_id_type=pl.DeviceIdType.MESH,
            )
    pl.semaphore_wait(barrier, rows + cols - 2)

    has = (me_col < cols - 1, me_row < rows - 1, me_col > 0, me_row > 0)
    there = ({"col": me_col + 1}, {"row": me_row + 1}, {"col": me_col - 1}, {"row": me_row - 1})

    for side in range(2):
        @pl.when(jnp.logical_not(has[side]))
        def _():
            back[side] = jnp.zeros(back.shape[1:], jnp.float32)

    for side in range(4):
        @pl.when(jnp.logical_not(has[side]))
        def _():
            for turn in range(ITERS):
                halo[turn, side] = jnp.zeros(halo.shape[2:], jnp.float32)

    def back_copy(seam):
        return pltpu.make_async_remote_copy(
            src_ref=scored.at[seam], dst_ref=back.at[seam],
            send_sem=back_send.at[seam], recv_sem=back_recv.at[seam],
            device_id=there[seam + 2], device_id_type=pl.DeviceIdType.MESH,
        )

    for seam in range(2):
        @pl.when(has[seam + 2])
        def _():
            back_copy(seam).start()

    for seam in range(2):
        @pl.when(has[seam + 2])
        def _():
            back_copy(seam).wait_send()

        @pl.when(has[seam])
        def _():
            back_copy(seam).wait_recv()

    def halo_copy(turn, side):
        return pltpu.make_async_remote_copy(
            src_ref=sent.at[turn], dst_ref=halo.at[turn, (side + 2) % 4],
            send_sem=halo_send.at[turn, side], recv_sem=halo_recv.at[turn, (side + 2) % 4],
            device_id=there[side], device_id_type=pl.DeviceIdType.MESH,
        )

    def row_copy(step):
        return pltpu.make_async_remote_copy(
            src_ref=part.at[0], dst_ref=row_parts.at[step - 1],
            send_sem=row_send.at[step - 1], recv_sem=row_recv.at[step - 1],
            device_id={"row": lax.rem(me_row + step, rows)},
            device_id_type=pl.DeviceIdType.MESH,
        )

    def col_copy(step):
        return pltpu.make_async_remote_copy(
            src_ref=part.at[1], dst_ref=col_parts.at[step - 1],
            send_sem=col_send.at[step - 1], recv_sem=col_recv.at[step - 1],
            device_id={"col": lax.rem(me_col + step, cols)},
            device_id_type=pl.DeviceIdType.MESH,
        )

    east = pltpu.roll(back[0, :, :CELLS], GV - 1, 1)
    south = pltpu.roll(back[1, :, :CELLS], CELLS - GV, 1)
    west = scored[0, :, :CELLS]
    north = scored[1, :, :CELLS]
    for seam in range(2):
        matches[seam] = back[seam, :3, CELLS : CELLS + P_SIZE]
    confs = [side[2:3, :] for side in (east, south, west, north)]
    turns = (GV - 1, CELLS - GV, CELLS - GV + 1, GV)
    component = lax.broadcasted_iota(jnp.int32, (8, CELLS), 0)
    forcing = confs[0] * east + confs[1] * south - confs[2] * west - confs[3] * north
    forcing = jnp.where(component < 2, forcing, 0.0)

    def operate(turn, vector):
        sent[turn] = vector
        for side in range(4):
            @pl.when(has[side])
            def _():
                halo_copy(turn, side).start()
        output = LAMBDA_REG * vector
        for index, gap in enumerate(GAPS):
            pull = springs[index : index + 1, :] * (vector - pltpu.roll(vector, CELLS - gap, 1))
            output = output + pull - pltpu.roll(pull, gap, 1)
        for side in range(4):
            @pl.when(has[side])
            def _():
                halo_copy(turn, side).wait_send()
                halo_copy(turn, (side + 2) % 4).wait_recv()
        for side in range(4):
            border = pltpu.roll(halo[turn, side], turns[side], 1)
            output = output + confs[side] * (vector - border)
        return output

    def lanes(values):
        folded = values[:, :128] + values[:, 128:]
        return jnp.sum(folded, axis=0, keepdims=True)

    basis = [forcing]
    for turn in range(ITERS):
        image = operate(turn, basis[-1])
        basis.append((image - CENTER * basis[-1]) * (1.0 / SPAN))

    pairs = [lanes(basis[(n + 0) // 2] * basis[(n + 1) // 2]) for n in range(2 * ITERS)]
    pad = part.shape[1] - len(pairs)
    total = jnp.concatenate(pairs + [jnp.zeros((pad, 128), jnp.float32)], axis=0)
    part[0] = total
    for step in range(1, rows):
        row_copy(step).start()
    for step in range(1, rows):
        row_copy(step).wait()
        total = total + row_parts[step - 1]
    part[1] = total
    for step in range(1, cols):
        col_copy(step).start()
    for step in range(1, cols):
        col_copy(step).wait()
        total = total + col_parts[step - 1]
    summed = jnp.sum(total, axis=1, keepdims=True)
    moments = [summed[n : n + 1] for n in range(2 * ITERS)]

    def inner(left, right):
        return sum(
            x * y * moments[i + j] for i, x in enumerate(left) for j, y in enumerate(right)
        )

    def apply(terms):
        kept = [CENTER * term for term in terms]
        raised = [SPAN * term for term in terms]
        middle = [low + high for low, high in zip(kept[1:], raised[:-1])]
        return kept[:1] + middle + raised[-1:]

    def combine(left, scale, right):
        joined = [x + scale * y for x, y in zip(left, right)]
        longer = left if len(left) > len(right) else [scale * y for y in right]
        return joined + longer[len(joined) :]

    one = jnp.ones((1, 1), jnp.float32)
    residual = [one]
    direction = [one]
    answer = []
    norm_now = moments[0]
    for iteration in range(ITERS):
        image = apply(direction)
        step_length = norm_now / inner(direction, image)
        answer = combine(answer, step_length, direction)
        if iteration + 1 < ITERS:
            residual = combine(residual, -step_length, image)
            norm_next = inner(residual, residual)
            direction = combine(residual, norm_next / norm_now, direction)
            norm_now = norm_next
    answer = sum(scale * vector for scale, vector in zip(answer, basis))
    shift[...] = answer[:2]


def mesh_call(scored, springs):
    rows = lax.axis_size("row")
    cols = lax.axis_size("col")
    vmem = pl.BlockSpec(memory_space=pltpu.VMEM)
    dma = pltpu.SemaphoreType.DMA
    return pl.pallas_call(
        functools.partial(mesh_kernel, (rows, cols)),
        out_shape=(
            jax.ShapeDtypeStruct((2, 3, P_SIZE), jnp.float32),
            jax.ShapeDtypeStruct((2, CELLS), jnp.float32),
        ),
        in_specs=[vmem, vmem],
        out_specs=(vmem, vmem),
        scratch_shapes=[
            pltpu.VMEM((2, 8, CELLS + 128), jnp.float32),
            pltpu.VMEM((ITERS, 4, 8, CELLS), jnp.float32),
            pltpu.VMEM((ITERS, 8, CELLS), jnp.float32),
            pltpu.VMEM((2, 8, 128), jnp.float32),
            pltpu.VMEM((rows - 1, 8, 128), jnp.float32),
            pltpu.VMEM((cols - 1, 8, 128), jnp.float32),
            dma((2,)),
            dma((2,)),
            dma((ITERS, 4)),
            dma((ITERS, 4)),
            dma((rows - 1,)),
            dma((rows - 1,)),
            dma((cols - 1,)),
            dma((cols - 1,)),
        ],
        compiler_params=pltpu.CompilerParams(collective_id=0, has_side_effects=True),
        name="mesh",
    )(scored, springs)


def body(patches, windows, candidates, live, edges, stiffness):
    given, cands = pass_call(patches[0, 0], candidates[0, 0])
    scored = match_call(live, cands, given, windows[0, 0])
    lower = jnp.minimum(edges[0, 0], edges[0, 1])
    gap = jnp.abs(edges[0, 0] - edges[0, 1])
    classes = jnp.array(GAPS + (0,) * 4)
    spring = jnp.where(gap[None, :] == classes[:, None], stiffness, 0.0)
    starts = (lower[:, None] == jnp.arange(CELLS)[None, :]).astype(jnp.float32)
    springs = jnp.dot(spring, starts, precision=PRECISE)
    matches, mesh_shift = mesh_call(scored, springs)
    return (matches[None, None], mesh_shift[None, None])


def solution(mesh):
    return jax.shard_map(
        body,
        mesh=mesh,
        in_specs=(
            P("row", "col", None, None, None, None),
            P("row", "col", None, None, None),
            P("row", "col", None, None, None),
            P(),
            P("row", None, "col"),
            P("row", "col"),
        ),
        out_specs=(P("row", "col", None, None, None), P("row", "col", None, None)),
        check_vma=False,
    )
```
